256 devices in a mesh: section: 4 (over y), fsdp: 8 (over x, z_hi), seq: 8 (over z_lo, core).
Axes of the slice: x: 4, y: 4, z: 8 (z_hi: 2, z_lo: 4; z = z_hi * 4 + z_lo), core: 2. Of those that a mesh axis runs over, the one named last changes fastest.
Arguments:
- hidden: bfloat16 [4, 16384, 8192], P('section', ('fsdp', 'seq')), may hold values from -6 to 6
- queries: bfloat16 [4, 16384, 4096], P('section', ('fsdp', 'seq')), may hold values from -6 to 6
- kv_weight: bfloat16 [4, 8192, 1024], P('section', ('fsdp', 'seq')), may hold values from -0.0625 to 0.0625
- readout: float32 [4, 4096], P('section'), may hold values from -6 to 6
- segments: int32 [8, 2048], P('fsdp'), may hold values from 0 to 3, never falling along the last dimension, each value on 1 to 1024 neighbouring positions
- block_mask: int32 [8, 16, 16], P('fsdp', 'seq'), may hold values 0 or 1
- response: int32 [16384], P(('fsdp', 'seq')), may hold values 0 or 1
Outputs:
- scores: float32 [4, 16384], P('section', ('fsdp', 'seq'))
- query_grad: bfloat16 [4, 16384, 4096], P('section', ('fsdp', 'seq'))
The draws below stay inside these ranges and needn't reach their ends.
All inputs are finite; a program needn't handle non-finite values. No bound on the sum of `block_mask` or of `response` on one device may be relied on, other than what follows from the above.
Results may differ from the reference program's by a relative error of at most 0.02.
Values may be sent and summed in bfloat16 or wider, within the bound.
No kernel may reach another device: no remote copies, remote signals or barrier semaphores. Data moves between devices by JAX's collectives and lax.ppermute only.
A program may use at most 128 MiB of HBM per device.

```python
import math
import jax
import jax.numpy as jnp
import numpy as np
from jax import lax

D = 8192
QH = 32
KVH = 4
HD = 128
BLK = 128
KVW = 512
QW = 4096
SEQ_LEN = 2048
NBLK = 16
SEQS = 8
TOKENS = 16384
N_SECTION = 4


def set_ends(values, stream_key, low, top_value):
    place = [jax.random.randint(jax.random.fold_in(stream_key, axis), (), 0, length) for axis, length in enumerate(values.shape)]
    main_axis = values.shape.index(max(values.shape))
    neighbour = place[:main_axis] + [(place[main_axis] + 1) % values.shape[main_axis]] + place[main_axis + 1:]
    return values.at[tuple(place)].set(low).at[tuple(neighbour)].set(top_value)


def steps_of(stream_key, dims, pieces, smallest, high):
    def one(position, shards_of):
        heights = jax.random.uniform(jax.random.fold_in(jax.random.fold_in(stream_key, 6), position), (shards_of,), jnp.float32, smallest / len(pieces), high / len(pieces))
        return jnp.repeat(jnp.exp(heights), dims[position] // shards_of).reshape((-1,) + (1,) * (len(dims) - position - 1))

    gain = one(*pieces[0])
    for cut in pieces[1:]:
        gain = gain * one(*cut)
    return gain


def split_up(number_of, total, most, slope):
    portions = [(1 << 20) // math.isqrt(grade ** slope) + 1 for grade in range(2, number_of + 1)]
    spare, given = total - most - (number_of - 1), [1] * (number_of - 1)
    while spare > 0:
        free = [i for i in range(number_of - 1) if given[i] < most]
        mass, remaining = sum([portions[i] for i in free]), spare
        for i in free:
            addition = min(most - given[i], max(1, remaining * portions[i] // mass), spare)
            given[i] = given[i] + addition
            spare = spare - addition
    return np.array([most] + given)


def ragged_sizes(key, number_of, total, reach, skew):
    if number_of == 2:
        one = jax.random.randint(key, (), max(1, total - reach), min(reach, total - 1) + 1)
        return jnp.stack([one, total - one])
    sizes = jnp.asarray(split_up(number_of, total, reach, skew), jnp.int32)
    pairs = (number_of - 1) // 2
    source_of, sink = sizes[1:1 + 2 * pairs:2], sizes[2:2 + 2 * pairs:2]
    slack = jnp.minimum(source_of - 1, reach - sink)
    passed = jax.random.randint(jax.random.fold_in(key, 1), (pairs,), 0, 1 << 20) % (slack + 1)
    sizes = sizes.at[1:1 + 2 * pairs:2].set(source_of - passed).at[2:2 + 2 * pairs:2].set(sink + passed)
    return sizes[jax.random.permutation(jax.random.fold_in(key, 2), number_of)]


def gaussian(rng, dims, spread, reach, split=(), held_as=jnp.bfloat16):
    factor_of = steps_of(rng, dims, split, -0.22, 0.18) if split else 1.0
    values = jax.random.normal(rng, dims, jnp.float32) * spread * factor_of
    return jnp.minimum(jnp.maximum(values, -reach), reach).astype(held_as)


def setup_inputs(seed: int = 0) -> dict:
    key_of = jax.random.split(jax.random.key(seed), 8)
    return {
        "hidden": gaussian(key_of[0], (N_SECTION, TOKENS, D), 1.0, 6.0, ((0, 4), (1, 64))),
        "queries": gaussian(key_of[1], (N_SECTION, TOKENS, QW), 1.0, 6.0, ((0, 4), (1, 64))),
        "kv_weight": gaussian(key_of[2], (N_SECTION, D, 2 * KVW), D ** -0.5, 0.0625, ((0, 4), (1, 64))),
        "readout": gaussian(key_of[3], (N_SECTION, QW), 1.0, 6.0, ((0, 4),), jnp.float32),
        "segments": jax.vmap(lambda own: jnp.searchsorted(jnp.cumsum(ragged_sizes(own, 4, SEQ_LEN, SEQ_LEN // 2, 1)), jnp.arange(SEQ_LEN), side="right"))(jax.random.split(key_of[4], SEQS)).reshape((SEQS, SEQ_LEN)).astype(jnp.int32),
        "block_mask": set_ends((jax.random.randint(key_of[5], (SEQS, NBLK, NBLK), 0, 4) < 3).astype(jnp.int32), jax.random.fold_in(key_of[5], 1), 0, 1),
        "response": set_ends((jax.random.randint(key_of[6], (TOKENS,), 0, 3) < 2).astype(jnp.int32), jax.random.fold_in(key_of[6], 1), 0, 1),
    }


penalty_weight = 0.5

def reference(hidden, queries, kv_weight, readout, segments, block_mask, response):
    group_size = QH // KVH
    kv_width = KVH * HD
    score_scale = 1.0 / math.sqrt(HD)
    projected = lax.map(lambda pair: jnp.dot(pair[0], pair[1], preferred_element_type=jnp.float32).astype(jnp.bfloat16), (hidden, kv_weight))
    positions = jnp.arange(SEQ_LEN, dtype=jnp.int32)
    blocks = positions // BLK
    same_block = blocks[:, None] == blocks[None, :]
    causal = positions[None, :] <= positions[:, None]

    def forward(item_index):
        section = item_index // SEQS
        sequence = item_index % SEQS
        row_start = (sequence * SEQ_LEN).astype(jnp.int32)
        kv_rows = lax.dynamic_slice_in_dim(lax.dynamic_index_in_dim(projected, section, 0, False), row_start, SEQ_LEN, 0).astype(jnp.float32)
        key_rows = kv_rows[:, :kv_width].reshape(SEQ_LEN, KVH, HD)
        values = kv_rows[:, kv_width:].reshape(SEQ_LEN, KVH, HD)
        query_rows = lax.dynamic_slice_in_dim(lax.dynamic_index_in_dim(queries, section, 0, False), row_start, SEQ_LEN, 0).astype(jnp.float32).reshape(SEQ_LEN, KVH, group_size, HD)
        doc_ids = lax.dynamic_index_in_dim(segments, sequence, 0, False)
        block_table = jnp.repeat(jnp.repeat(lax.dynamic_index_in_dim(block_mask, sequence, 0, False), BLK, axis=0), BLK, axis=1)
        allowed = (doc_ids[:, None] == doc_ids[None, :]) & causal & ((block_table == 1) | same_block)
        logits = jnp.einsum('ikgd,jkd->kgij', query_rows, key_rows) * score_scale
        weights = jnp.where(allowed[None, None], jnp.exp(logits), 0.0)
        denominator = jnp.transpose(lax.optimization_barrier(jnp.sum(weights, axis=-1)), (2, 0, 1))
        rounded = weights.astype(jnp.bfloat16)
        summed = jnp.einsum('kgij,jkd->ikgd', rounded.astype(jnp.float32), values)
        attended = summed / denominator[..., None]
        read_gains = lax.dynamic_index_in_dim(readout, section, 0, False).astype(jnp.float32).reshape(KVH, group_size, HD)
        head_scores = lax.optimization_barrier(jnp.sum(attended * read_gains, axis=-1))
        return (weights, rounded, denominator, head_scores, key_rows, values, read_gains)

    def score_of(item_index):
        head_scores = forward(item_index)[3]
        return lax.optimization_barrier(jnp.sum(head_scores, axis=(1, 2)))
    items = jnp.arange(N_SECTION * SEQS, dtype=jnp.int32)
    scores = lax.map(score_of, items).reshape(N_SECTION, TOKENS)
    live_rows = response.astype(jnp.float32)
    actor_grad = live_rows * (penalty_weight * (scores[0] - scores[1]) - (scores[2] - scores[3]))
    critic_grad = live_rows * (scores[3] - scores[2])
    no_grad = jnp.zeros_like(live_rows)
    loss_grad = jnp.stack([actor_grad, no_grad, no_grad, critic_grad])

    def grad_of(item_index):
        weights, rounded, denominator, head_scores, key_rows, values, read_gains = forward(item_index)
        section = item_index // SEQS
        sequence = item_index % SEQS
        grad_rows = lax.dynamic_slice_in_dim(lax.dynamic_index_in_dim(loss_grad, section, 0, False), (sequence * SEQ_LEN).astype(jnp.int32), SEQ_LEN, 0)
        value_gain = jnp.einsum('jkd,kgd->jkg', values, read_gains)
        scaled = (weights * jnp.transpose(value_gain, (1, 2, 0))[:, :, None, :]).astype(jnp.bfloat16)
        first_sum = jnp.einsum('kgij,jkd->ikgd', scaled.astype(jnp.float32), key_rows)
        second_sum = jnp.einsum('kgij,jkd->ikgd', rounded.astype(jnp.float32), key_rows)
        factor = score_scale * grad_rows[:, None, None] / denominator
        result = factor[..., None] * (first_sum - head_scores[..., None] * second_sum)
        return result.reshape(SEQ_LEN, QH * HD).astype(jnp.bfloat16)
    query_grad = lax.map(grad_of, items).reshape(N_SECTION, TOKENS, QH * HD)
    return (scores, query_grad)
```

```python
import functools
import math

import jax
import jax.numpy as jnp
import numpy as np
from jax import lax
from jax.experimental import pallas as pl
from jax.experimental.pallas import tpu as pltpu
from jax.sharding import PartitionSpec as P

QH = 32
KVH = 4
HD = 128
BLK = 128
GROUP = QH // KVH
KVW = KVH * HD
HALF = KVW // 2
WINDOW = 12 * BLK
NEG = -1e30
PLANE = ("fsdp", "seq")
X_SIZE, Z_SIZE, Z_LOW = 4, 8, 4
F32 = jnp.float32
BF16 = jnp.bfloat16

penalty_weight = 0.5


def flat(x, z, core):
    return (x * (Z_SIZE // Z_LOW) + z // Z_LOW) * (2 * Z_LOW) + (z % Z_LOW) * 2 + core


def plane_permute(value, target):
    pairs = []
    for x in range(X_SIZE):
        for z in range(Z_SIZE):
            for core in range(2):
                there = target(x, z, core)
                if there is not None:
                    pairs.append((flat(x, z, core), flat(*there)))
    return lax.ppermute(value, PLANE, pairs)


def x_shift(value, step):
    return plane_permute(value, lambda x, z, core: ((x + step) % X_SIZE, z, core))


def z_shift(value, step):
    return plane_permute(value, lambda x, z, core: (x, (z + step) % Z_SIZE, core))


def core_swap(value):
    return plane_permute(value, lambda x, z, core: (x, z, 1 - core))


def next_chip(value):
    return plane_permute(value, lambda x, z, core: (x, z + 1, core) if z % Z_LOW < Z_LOW - 1 else None)


def pack_kernel(w_ref, r_ref, a_ref, b_ref):
    a_ref[:BLK, :] = w_ref[:, :HALF]
    b_ref[...] = w_ref[:, HALF:KVW]
    gains = []
    for kv in range(KVH):
        wv = w_ref[:, KVW + kv * HD : KVW + (kv + 1) * HD].astype(F32)
        gains.append(
            lax.dot_general(
                r_ref[kv * GROUP : (kv + 1) * GROUP, :],
                wv,
                (((1,), (1,)), ((), ())),
                precision=lax.Precision.HIGHEST,
                preferred_element_type=F32,
            )
        )
    a_ref[BLK:, :HD] = jnp.concatenate(gains[:2], axis=0).astype(BF16)
    a_ref[BLK:, HD:] = jnp.concatenate(gains[2:], axis=0).astype(BF16)


def pack_weights(weight, gains):
    return pl.pallas_call(
        pack_kernel,
        out_shape=(
            jax.ShapeDtypeStruct((BLK + 16, HALF), BF16),
            jax.ShapeDtypeStruct((BLK, HALF), BF16),
        ),
        name="pack",
    )(weight, gains)


def stack_kernel(*refs):
    for i, ref in enumerate(refs[:-1]):
        refs[-1][i] = ref[...]


def stack(blocks):
    return pl.pallas_call(
        stack_kernel,
        out_shape=jax.ShapeDtypeStruct((len(blocks),) + blocks[0].shape, BF16),
        name="stack",
    )(*blocks)


def project_kernel(steps, with_gain, place_s, *refs):
    width = len(steps[0])
    own, refs = refs[:width], refs[width:]
    other, refs = refs[:width], refs[width:]
    count = 1 + max(a for step in steps for a, _ in step)
    weights, outs = refs[:count], refs[count:]
    now = pl.program_id(0)

    @pl.when(now == 0)
    def _():
        for out in outs:
            out[...] = jnp.zeros_like(out)

    hidden = [jnp.concatenate([ref[...] for ref in blocks], axis=1) for blocks in (own, other)]
    for number, step in enumerate(steps):

        @pl.when(now == number)
        def _():
            w = jnp.concatenate([weights[a][i, :BLK, :] for a, i in step], axis=0)
            if with_gain:
                wu = jnp.concatenate(
                    [jnp.concatenate([weights[a][i, BLK:, :HD], weights[a][i, BLK:, HD:]], axis=0) for a, i in step],
                    axis=1,
                )
            for side, h in enumerate(hidden):
                outs[0][side] += jnp.dot(h, w, preferred_element_type=F32)
                if with_gain:
                    outs[1][side] += lax.dot_general(wu, h, (((1,), (1,)), ((), ())), preferred_element_type=F32)


def project(place, own, other, weights, steps, column, with_gain):
    rows = own.shape[0]
    width = len(steps[0])
    shapes = [(2, rows, HALF)] + ([(2, QH, rows)] if with_gain else [])

    def whole(shape):
        return pl.BlockSpec(shape, lambda i, place, n=len(shape): (0,) * n)

    columns = [pl.BlockSpec((rows, BLK), lambda i, place, t=t: (0, column(i, t, place))) for t in range(width)]
    return pl.pallas_call(
        functools.partial(project_kernel, steps, with_gain),
        out_shape=[jax.ShapeDtypeStruct(s, F32) for s in shapes],
        grid_spec=pltpu.PrefetchScalarGridSpec(
            num_scalar_prefetch=1,
            grid=(len(steps),),
            in_specs=columns * 2 + [whole(w.shape) for w in weights],
            out_specs=[whole(s) for s in shapes],
        ),
        compiler_params=pltpu.CompilerParams(dimension_semantics=("arbitrary",)),
        cost_estimate=pl.CostEstimate(
            flops=2 * 2 * rows * len(steps) * width * BLK * (HALF + QH),
            bytes_accessed=4 * rows * len(steps) * width * BLK,
            transcendentals=0,
        ),
        name="project",
    )(place, *([own] * width), *([other] * width), *weights)


def a_column(step, t, place):
    spot = 2 * step + t // 4
    away = (spot + 1) // 2 * (1 - 2 * (spot % 2))
    x = (place[0] + (0, 3, 1, 2)[t % 4]) % X_SIZE
    return (x * Z_SIZE + (place[1] + away + Z_SIZE) % Z_SIZE) * 2 + place[2]


def b_column(step, t, place):
    away = jnp.where(step == 1, 3, jnp.where(step == 2, 1, jnp.where(step == 3, 2, 0)))
    z = (place[1] + (0, 7, 6, 5, 4, 1, 2, 3)[t]) % Z_SIZE
    return (((place[0] + away) % X_SIZE) * Z_SIZE + z) * 2 + place[2]


A_STEPS = tuple(tuple((2 * s + t // 4, t % 4) for t in range(8)) for s in range(3)) + (
    tuple((6, t) for t in range(4)) + ((7, 0), (7, 1), (8, 0), (8, 1)),
)
B_STEPS = tuple(tuple((s, t) for t in range(8)) for s in range(3)) + (tuple((3 + t // 4, t % 4) for t in range(8)),)


def finish_kernel(heads, k_ref, u_ref, rk_ref, ru_ref, o_ref):
    rows = k_ref.shape[1]
    o_ref[:rows, :] = (k_ref[0] + rk_ref[...]).astype(BF16)
    u = u_ref[0] + ru_ref[...]
    high = u.astype(BF16)
    low = (u - high.astype(F32)).astype(BF16)
    for n, kv in enumerate(heads):
        group = slice(kv * GROUP, (kv + 1) * GROUP)
        o_ref[rows:, n * HD : (n + 1) * HD] = jnp.concatenate(
            [part[group, i * BLK : (i + 1) * BLK].astype(F32) for part in (high, low) for i in range(2)], axis=0
        ).astype(BF16)


def finish(heads, k, u, rk, ru):
    rows = k.shape[1]
    return pl.pallas_call(
        functools.partial(finish_kernel, heads),
        out_shape=jax.ShapeDtypeStruct((rows + 4 * GROUP, HALF), BF16),
        name="finish",
    )(k, u, rk, ru)


def attention_kernel(
    seg_s, mask_s, place_s, q_ref, *refs
):
    same_refs, other_refs = refs[:3], refs[3:6]
    segq_ref, segk_ref, x_ref, sc_ref = refs[6:10]
    kall, uall, kc, uc, bias, p_s, den_a, rho_a, rho_b, acc, idx, cnt = refs[10:]
    kv = pl.program_id(0)
    log_scale = np.float32(math.log2(math.e) / math.sqrt(HD))
    scale = np.float32(1.0 / math.sqrt(HD))
    chip = place_s[1] % Z_LOW
    core = place_s[2]
    rows2 = 2 * BLK

    for side, side_refs in enumerate((same_refs, other_refs)):
        for back, ref in enumerate(side_refs):
            where = (2 - back) * 2 * rows2 + (core if side == 0 else 1 - core) * rows2
            kall[pl.ds(pl.multiple_of(where, rows2), rows2), :] = ref[:rows2, :]
            extra = ref[rows2:, :].astype(F32)
            for i in range(2):
                uall[:, pl.ds(pl.multiple_of(where + i * BLK, BLK), BLK)] = (
                    extra[i * GROUP : (i + 1) * GROUP] + extra[(2 + i) * GROUP : (3 + i) * GROUP]
                )

    @pl.when(kv == 0)
    def _():
        sc_ref[...] = jnp.zeros_like(sc_ref)
        for b in range(2):
            diagonal = 8 + 2 * core + b
            first = seg_s[(4 * chip + 2 * core + b) * BLK]

            def scan(l, n):
                block = 4 * (chip - 2) + l
                held = jnp.maximum(block, 0)
                on = (l == diagonal) | (
                    (block >= 0) & (mask_s[b * 16 + held] == 1) & (seg_s[held * BLK + BLK - 1] == first)
                )

                @pl.when(on)
                def _():
                    idx[b * 16 + n] = l

                return n + on.astype(jnp.int32)

            n = lax.fori_loop(0, diagonal + 1, scan, jnp.int32(0))
            cnt[b] = n

            def fill(t, _):
                l = idx[b * 16 + t]
                key_docs = segk_ref[0:1, pl.ds(pl.multiple_of(l * BLK, BLK), BLK)]
                query_docs = segq_ref[pl.ds(b * BLK, BLK), :]
                i = lax.broadcasted_iota(jnp.int32, (BLK, BLK), 0)
                j = lax.broadcasted_iota(jnp.int32, (BLK, BLK), 1)
                allowed = (query_docs == key_docs) & ((l != diagonal) | (j <= i))
                bias[b, :, pl.ds(pl.multiple_of(t * BLK, BLK), BLK)] = jnp.where(allowed, 0.0, NEG).astype(F32)
                return 0

            lax.fori_loop(0, n, fill, 0)

            @pl.when(n % 2 == 1)
            def _():
                bias[b, :, pl.ds(pl.multiple_of(n * BLK, BLK), BLK)] = jnp.full((BLK, BLK), NEG, F32)

    for b in range(2):
        n = cnt[b]
        chunks = (n + 1) // 2

        def compact(t, _):
            l = idx[b * 16 + t]
            d = pl.multiple_of(t * BLK, BLK)
            s = pl.multiple_of(l * BLK, BLK)
            kc[pl.ds(d, BLK), :] = kall[pl.ds(s, BLK), :]
            uc[:, pl.ds(d, BLK)] = uall[:, pl.ds(s, BLK)]
            return 0

        lax.fori_loop(0, n, compact, 0)

        @pl.when(n % 2 == 1)
        def _():
            d = pl.multiple_of(n * BLK, BLK)
            kc[pl.ds(d, BLK), :] = jnp.zeros((BLK, HD), BF16)
            uc[:, pl.ds(d, BLK)] = jnp.zeros((GROUP, BLK), F32)

        den_a[...] = jnp.zeros_like(den_a)
        rho_a[...] = jnp.zeros_like(rho_a)
        acc[...] = jnp.zeros_like(acc)
        rows = pl.ds(b * BLK, BLK)

        def weigh(c, _):
            ks = pl.ds(pl.multiple_of(c * 2 * BLK, 2 * BLK), 2 * BLK)
            keys = kc[ks, :]
            shut = bias[b, :, ks]
            for g in range(GROUP):
                q = q_ref[rows, g * HD : (g + 1) * HD]
                s = lax.dot_general(q, keys, (((1,), (1,)), ((), ())), preferred_element_type=F32)
                p = jnp.exp2(s * log_scale + shut)
                p_s[g, :, ks] = p
                pu = p * uc[g : g + 1, ks]
                den_a[g] += p[:, :BLK] + p[:, BLK:]
                rho_a[g] += pu[:, :BLK] + pu[:, BLK:]
            return 0

        lax.fori_loop(0, chunks, weigh, 0)
        total = jnp.zeros((BLK, 1), F32)
        for g in range(GROUP):
            den = jnp.sum(den_a[g], axis=-1, keepdims=True)
            rho = jnp.sum(rho_a[g], axis=-1, keepdims=True) / den
            total += rho
            rho_b[g] = jnp.broadcast_to(rho, (BLK, HD))
            den_a[g] = jnp.broadcast_to(scale / den, (BLK, HD))
        sc_ref[rows, :] += jnp.broadcast_to(total, (BLK, HD))

        def spread(c, _):
            ks = pl.ds(pl.multiple_of(c * 2 * BLK, 2 * BLK), 2 * BLK)
            keys = kc[ks, :]
            for g in range(GROUP):
                r = rho_b[g]
                p = p_s[g, :, ks]
                u = uc[g : g + 1, ks]
                w = jnp.concatenate(
                    [p[:, :BLK] * (u[:, :BLK] - r), p[:, BLK:] * (u[:, BLK:] - r)], axis=1
                ).astype(BF16)
                acc[g] += jnp.dot(w, keys, preferred_element_type=F32)
            return 0

        lax.fori_loop(0, chunks, spread, 0)
        for g in range(GROUP):
            x_ref[rows, g * HD : (g + 1) * HD] = (acc[g] * den_a[g]).astype(BF16)


def attention(half, docs, mask, place, queries, same, other, query_docs, key_docs):
    rows = queries.shape[0]
    held = same[0].shape[0]
    head_block = pl.BlockSpec((held, HD), lambda i, *_: (0, i))
    return pl.pallas_call(
        attention_kernel,
        out_shape=(
            jax.ShapeDtypeStruct((rows, QH * HD // 2), BF16),
            jax.ShapeDtypeStruct((rows, HD), F32),
        ),
        grid_spec=pltpu.PrefetchScalarGridSpec(
            num_scalar_prefetch=3,
            grid=(KVH // 2,),
            in_specs=[pl.BlockSpec((rows, GROUP * HD), lambda i, *_: (0, i + half * KVH // 2))]
            + [head_block] * 6
            + [
                pl.BlockSpec((rows, HD), lambda i, *_: (0, 0)),
                pl.BlockSpec((8, WINDOW), lambda i, *_: (0, 0)),
            ],
            out_specs=[
                pl.BlockSpec((rows, GROUP * HD), lambda i, *_: (0, i)),
                pl.BlockSpec((rows, HD), lambda i, *_: (0, 0)),
            ],
            scratch_shapes=[
                pltpu.VMEM((WINDOW, HD), BF16),
                pltpu.VMEM((GROUP, WINDOW), F32),
                pltpu.VMEM((WINDOW, HD), BF16),
                pltpu.VMEM((GROUP, WINDOW), F32),
                pltpu.VMEM((2, BLK, WINDOW), F32),
                pltpu.VMEM((GROUP, BLK, WINDOW), F32),
                pltpu.VMEM((GROUP, BLK, BLK), F32),
                pltpu.VMEM((GROUP, BLK, BLK), F32),
                pltpu.VMEM((GROUP, BLK, BLK), F32),
                pltpu.VMEM((GROUP, BLK, HD), F32),
                pltpu.SMEM((32,), jnp.int32),
                pltpu.SMEM((2,), jnp.int32),
            ],
        ),
        compiler_params=pltpu.CompilerParams(dimension_semantics=("arbitrary",)),
        cost_estimate=pl.CostEstimate(flops=5 * 10**9, bytes_accessed=3 << 20, transcendentals=5 * 10**6),
        name="attention",
    )(docs, mask, place, queries, *same, *other, query_docs, key_docs)


def gathered_weights(weight, gains):
    part_a, part_b = pack_weights(weight, gains)
    a_own = stack([part_a, x_shift(part_a, 1), x_shift(part_a, -1), x_shift(part_a, 2)])
    b_back = [part_b]
    b_ahead = [part_b]
    for _ in range(3):
        b_back.append(z_shift(b_back[-1], 1))
        b_ahead.append(z_shift(b_ahead[-1], -1))
    b_back.append(z_shift(b_back[-1], 1))
    b_own = stack(b_back + b_ahead[1:])
    all_a = [a_own]
    a_back, a_ahead = a_own, a_own
    for _ in range(3):
        a_back, a_ahead = z_shift(a_back, 1), z_shift(a_ahead, -1)
        all_a += [a_back, a_ahead]
    all_a += [z_shift(a_back[:2], 1), z_shift(a_ahead[2:], -1)]
    b_one, b_three = x_shift(b_own, 1), x_shift(b_own, -1)
    all_b = [b_own, b_one, b_three, x_shift(b_one[:4], 1), x_shift(b_three[4:], -1)]
    return all_a, all_b


def key_window(packed):
    back_one = next_chip(packed)
    same = [packed, back_one, next_chip(back_one)]
    return same, [core_swap(v) for v in same]


def on_device(hidden, queries, kv_weight, readout, segments, block_mask, response):
    rows = hidden.shape[1]
    fsdp = lax.axis_index("fsdp")
    seq = lax.axis_index("seq")
    chip, core = seq // 2, seq % 2
    place = jnp.stack([fsdp // 2, (fsdp % 2) * Z_LOW + chip, core])
    other = core_swap(hidden[0])
    all_a, all_b = gathered_weights(kv_weight[0], readout[0].reshape(QH, HD))
    keys_a, gains = project(place, hidden[0], other, all_a, A_STEPS, a_column, True)
    gains_in = core_swap(gains[1])
    windows = [key_window(finish((0, 1), keys_a, gains, core_swap(keys_a[1]), gains_in))]
    (keys_b,) = project(place, hidden[0], other, all_b, B_STEPS, b_column, False)
    windows.append(key_window(finish((2, 3), keys_b, gains, core_swap(keys_b[1]), gains_in)))

    docs = segments[0]
    padded = jnp.concatenate([jnp.full((WINDOW - 2 * rows,), -1, jnp.int32), docs])
    key_docs = jnp.broadcast_to(lax.dynamic_slice_in_dim(padded, chip * 2 * rows, WINDOW)[None], (8, WINDOW))
    query_docs = jnp.broadcast_to(lax.dynamic_slice_in_dim(docs, seq * rows, rows)[:, None], (rows, HD))
    parts = [
        attention(half, docs, block_mask[0].reshape(-1), place, queries[0], *windows[half], query_docs, key_docs)
        for half in range(2)
    ]
    scores = parts[0][1][:, 0] + parts[1][1][:, 0]
    near = lax.ppermute(scores, "section", [(1, 0), (2, 3)])
    reward = lax.ppermute(scores, "section", [(2, 0)])
    critic = lax.ppermute(scores, "section", [(3, 0)])
    section = lax.axis_index("section")
    actor_term = penalty_weight * (scores - near) - (reward - critic)
    critic_term = scores - near
    live = response.astype(F32)
    loss_grad = live * jnp.where(section == 0, actor_term, jnp.where(section == 3, critic_term, 0.0))
    unscaled = jnp.concatenate([parts[0][0], parts[1][0]], axis=1)
    query_grad = (unscaled.astype(F32) * loss_grad[:, None]).astype(BF16)
    return (scores[None, :], query_grad[None])


def solution(mesh):
    placed = (
        P("section", ("fsdp", "seq"), None),
        P("section", ("fsdp", "seq"), None),
        P("section", ("fsdp", "seq"), None),
        P("section", None),
        P("fsdp", None),
        P("fsdp", "seq", None),
        P(("fsdp", "seq")),
    )
    return jax.shard_map(
        on_device,
        mesh=mesh,
        in_specs=placed,
        out_specs=(P("section", ("fsdp", "seq")), P("section", ("fsdp", "seq"), None)),
        check_vma=False,
    )
```

```python
import functools
import math

import jax
import jax.numpy as jnp
import numpy as np
from jax import lax
from jax.experimental import pallas as pl
from jax.experimental.pallas import tpu as pltpu
from jax.sharding import PartitionSpec as P

QH = 32
KVH = 4
HD = 128
BLK = 128
GROUP = QH // KVH
KVW = KVH * HD
HALF = KVW // 2
WINDOW = 12 * BLK
HEADS = GROUP * HD
ZORDER = (0, 7, 1, 6, 2, 5, 3, 4)
NEG = -1e30
PLANE = ("fsdp", "seq")
X_SIZE, Z_SIZE, Z_LOW = 4, 8, 4
F32 = jnp.float32
BF16 = jnp.bfloat16

penalty_weight = 0.5


def flat(x, z, core):
    return (x * (Z_SIZE // Z_LOW) + z // Z_LOW) * (2 * Z_LOW) + (z % Z_LOW) * 2 + core


def plane_permute(value, target):
    pairs = []
    for x in range(X_SIZE):
        for z in range(Z_SIZE):
            for core in range(2):
                there = target(x, z, core)
                if there is not None:
                    pairs.append((flat(x, z, core), flat(*there)))
    return lax.ppermute(value, PLANE, pairs)


def x_shift(value, step):
    return plane_permute(value, lambda x, z, core: ((x + step) % X_SIZE, z, core))


def z_shift(value, step):
    return plane_permute(value, lambda x, z, core: (x, (z + step) % Z_SIZE, core))


def core_swap(value):
    return plane_permute(value, lambda x, z, core: (x, z, 1 - core))


def limit(mib):
    return pltpu.CompilerParams(vmem_limit_bytes=mib << 20)


def pack_kernel(place_s, w_ref, r_ref, a_ref, b_ref):
    core = place_s[2]
    order = [2 * core, 2 * core + 1, 2 - 2 * core, 3 - 2 * core]

    def lanes(kv):
        return pl.ds(pl.multiple_of(kv * HD, HD), HD)

    for n in range(2):
        a_ref[:, n * HD : (n + 1) * HD] = w_ref[:, lanes(order[2 * n])]
        b_ref[:BLK, n * HD : (n + 1) * HD] = w_ref[:, lanes(order[2 * n + 1])]
    gains = []
    for kv in order:
        gains.append(
            lax.dot_general(
                r_ref[pl.ds(pl.multiple_of(kv * GROUP, GROUP), GROUP), :],
                w_ref[:, pl.ds(pl.multiple_of(KVW + kv * HD, HD), HD)].astype(F32),
                (((1,), (1,)), ((), ())),
                precision=lax.Precision.HIGHEST,
                preferred_element_type=F32,
            )
        )
    b_ref[BLK:, :HD] = jnp.concatenate(gains[:2], axis=0).astype(BF16)
    b_ref[BLK:, HD:] = jnp.concatenate(gains[2:], axis=0).astype(BF16)


def pack_weights(place, weight, gains):
    def whole(shape):
        return pl.BlockSpec(shape, lambda i, place, n=len(shape): (0,) * n)

    shapes = [(BLK, HALF), (BLK + 16, HALF)]
    return pl.pallas_call(
        pack_kernel,
        out_shape=[jax.ShapeDtypeStruct(shape, BF16) for shape in shapes],
        grid_spec=pltpu.PrefetchScalarGridSpec(
            num_scalar_prefetch=1,
            grid=(1,),
            in_specs=[whole(weight.shape), whole(gains.shape)],
            out_specs=[whole(shape) for shape in shapes],
        ),
        compiler_params=limit(8),
        name="pack",
    )(place, weight, gains)


def stack_kernel(*refs):
    for i, ref in enumerate(refs[:-1]):
        refs[-1][i] = ref[...]


def stack(blocks):
    return pl.pallas_call(
        stack_kernel,
        out_shape=jax.ShapeDtypeStruct((len(blocks),) + blocks[0].shape, BF16),
        compiler_params=limit(8),
        name="stack",
    )(*blocks)


def project_kernel(place_s, own_ref, other_ref, *refs):
    all_a, all_b, refs = refs[:9], refs[9:14], refs[14:]
    mine_ref, theirs_ref, acc, gain_acc = refs
    now = pl.program_id(0)
    core = place_s[2]
    rows = own_ref.shape[0]
    tokens = 2 * rows
    for number in range(X_SIZE):

        @pl.when(now == number)
        def _():
            units = [(all_a[p], number) for p in range(7)] + [(all_a[7 + number // 2], number % 2)]
            w_a = jnp.concatenate([ref[i] for ref, i in units], axis=0)
            units = [(all_b[number + (i // 4 if number == 3 else 0)], i % (4 if number == 3 else 8)) for i in range(8)]
            w_b = jnp.concatenate([ref[i, :BLK, :] for ref, i in units], axis=0)
            wu = jnp.concatenate(
                [jnp.concatenate([ref[i, BLK:, :HD], ref[i, BLK:, HD:]], axis=0) for ref, i in units], axis=1
            )
            for side, ref in enumerate((own_ref, other_ref)):
                pieces = []
                for away in ZORDER:
                    z = (place_s[1] + away) % Z_SIZE
                    pieces.append(ref[:, pl.ds(pl.multiple_of((2 * z + core) * BLK, BLK), BLK)])
                h = jnp.concatenate(pieces, axis=1)
                for n, w in enumerate((w_a, w_b)):
                    part = jnp.dot(h, w, preferred_element_type=F32)
                    acc[side, n] = part if number == 0 else acc[side, n] + part
                part = lax.dot_general(wu, h, (((1,), (1,)), ((), ())), preferred_element_type=F32)
                gain_acc[side] = part if number == 0 else gain_acc[side] + part

    @pl.when(now == X_SIZE - 1)
    def _():
        for side in range(2):
            place_of = core if side == 0 else 1 - core
            for n, ref in enumerate((mine_ref, theirs_ref)):
                lanes = slice(n * HD, (n + 1) * HD)
                for half in range(2):
                    spot = pl.multiple_of(half * tokens + place_of * rows, rows)
                    ref[pl.ds(spot, rows), :] = acc[side, half, :, lanes]
                for i in range(rows // BLK):
                    spot = pl.multiple_of(2 * tokens + (2 * place_of + i) * 16, 16)
                    ref[pl.ds(spot, 16), :] = gain_acc[side, n * 16 : (n + 1) * 16, i * BLK : (i + 1) * BLK]


def project(place, own, other, weights):
    rows = own.shape[0]
    tokens = 2 * rows
    held = 2 * tokens + tokens // BLK * 16
    wide = 2 * Z_SIZE * BLK

    def whole(shape):
        return pl.BlockSpec(shape, lambda i, place, n=len(shape): (0,) * n)

    def column(i, place):
        return (0, (place[0] + jnp.where(i == 1, 3, jnp.where(i == 2, 1, jnp.where(i == 3, 2, 0)))) % X_SIZE)

    return pl.pallas_call(
        project_kernel,
        out_shape=[jax.ShapeDtypeStruct((held, HD), F32)] * 2,
        grid_spec=pltpu.PrefetchScalarGridSpec(
            num_scalar_prefetch=1,
            grid=(X_SIZE,),
            in_specs=[pl.BlockSpec((rows, wide), column)] * 2 + [whole(w.shape) for w in weights],
            out_specs=[whole((held, HD))] * 2,
            scratch_shapes=[pltpu.VMEM((2, 2, rows, HALF), F32), pltpu.VMEM((2, QH, rows), F32)],
        ),
        compiler_params=limit(28),
        cost_estimate=pl.CostEstimate(
            flops=2 * tokens * 32 * BLK * KVW, bytes_accessed=8 * tokens * 32 * BLK, transcendentals=0
        ),
        name="project",
    )(place, own, other, *weights)


def finish_kernel(mine_ref, in_ref, a_ref, b_ref):
    tokens = b_ref.shape[0]
    a_ref[:tokens, :] = (mine_ref[:tokens, :] + in_ref[:tokens, :]).astype(BF16)
    b_ref[...] = (mine_ref[tokens : 2 * tokens, :] + in_ref[tokens : 2 * tokens, :]).astype(BF16)
    u = mine_ref[2 * tokens :, :] + in_ref[2 * tokens :, :]
    high = u.astype(BF16)
    a_ref[tokens : tokens + 64, :] = high
    a_ref[tokens + 64 :, :] = (u - high.astype(F32)).astype(BF16)


def finish(mine, received):
    tokens = 4 * BLK
    return pl.pallas_call(
        finish_kernel,
        out_shape=(
            jax.ShapeDtypeStruct((tokens + 128, HD), BF16),
            jax.ShapeDtypeStruct((tokens, HD), BF16),
        ),
        compiler_params=limit(8),
        name="finish",
    )(mine, received)


def attention_kernel(half, seg_s, mask_s, mask_in_s, place_s, docs_ref, *refs):
    queries, refs = refs[:2], refs[2:]
    key_refs, refs = refs[:3], refs[3:]
    gain_refs, refs = refs[:3], refs[3:]
    if half:
        before_ref, refs = refs[0], refs[1:]
    outs, sc_ref, refs = refs[:2], refs[2], refs[3:]
    kc, uc, bias, p_s, den_a, rho_a, rho_b, acc, ub, idx = refs
    log_scale = np.float32(math.log2(math.e) / math.sqrt(HD))
    scale = np.float32(1.0 / math.sqrt(HD))
    chip = place_s[1] % Z_LOW
    core = place_s[2]
    tokens = 4 * BLK
    sc_ref[...] = before_ref[...] if half else jnp.zeros_like(sc_ref)
    ii = lax.broadcasted_iota(jnp.int32, (BLK, BLK), 0)
    jj = lax.broadcasted_iota(jnp.int32, (BLK, BLK), 1)

    for side in range(2):
        side_core = core if side == 0 else 1 - core
        mask = (mask_s, mask_in_s)[side]
        for b in range(2):
            inner = 2 * side_core + b
            block = 4 * chip + inner
            first = seg_s[block * BLK]
            row_docs = jnp.broadcast_to(docs_ref[pl.ds(block, 1), :], (BLK, BLK)).astype(F32).T.astype(jnp.int32)

            def fetch(n, ref, gain_ref, at):
                d = pl.multiple_of(n * BLK, BLK)
                kc[pl.ds(d, BLK), :] = ref[pl.ds(pl.multiple_of(at * BLK, BLK), BLK), :]
                spot = tokens + at * 16
                high = gain_ref[pl.ds(pl.multiple_of(spot, 16), 16), :].astype(F32)
                low = gain_ref[pl.ds(pl.multiple_of(spot + 64, 16), 16), :].astype(F32)
                uc[:, pl.ds(d, BLK)] = (high + low)[half * GROUP : (half + 1) * GROUP]

            n = jnp.int32(0)
            for back in (2, 1, 0):

                def scan(at, n, back=back):
                    key_block = 4 * (chip - back) + at
                    held = jnp.maximum(key_block, 0)
                    on = (key_block == block) | (
                        (key_block >= 0)
                        & (key_block < block)
                        & (mask[b * 16 + held] == 1)
                        & (seg_s[held * BLK + BLK - 1] == first)
                    )

                    @pl.when(on)
                    def _():
                        idx[n] = held
                        fetch(n, key_refs[back], gain_refs[back], at)

                    return n + on.astype(jnp.int32)

                n = lax.fori_loop(0, 4, scan, n)

            def fill(t, _):
                key_docs = docs_ref[pl.ds(idx[t], 1), :]
                bias[:, pl.ds(pl.multiple_of(t * BLK, BLK), BLK)] = jnp.where(row_docs == key_docs, 0.0, NEG)
                return 0

            lax.fori_loop(0, n - 1, fill, 0)
            last = pl.ds(pl.multiple_of((n - 1) * BLK, BLK), BLK)
            key_docs = docs_ref[pl.ds(block, 1), :]
            bias[:, last] = jnp.where((row_docs == key_docs) & (jj <= ii), 0.0, NEG)

            @pl.when(n % 2 == 1)
            def _():
                d = pl.ds(pl.multiple_of(n * BLK, BLK), BLK)
                bias[:, d] = jnp.full((BLK, BLK), NEG, F32)
                kc[d, :] = jnp.zeros((BLK, HD), BF16)
                uc[:, d] = jnp.zeros((GROUP, BLK), F32)

            chunks = (n + 1) // 2
            ub[...] = uc[...].astype(BF16)
            den_a[...] = jnp.zeros_like(den_a)
            rho_a[...] = jnp.zeros_like(rho_a)
            acc[...] = jnp.zeros_like(acc)
            rows = slice(b * BLK, (b + 1) * BLK)

            def weigh(c, _):
                ks = pl.ds(pl.multiple_of(c * 2 * BLK, 2 * BLK), 2 * BLK)
                keys = kc[ks, :]
                shut = bias[:, ks]
                for g in range(GROUP):
                    q = queries[side][rows, g * HD : (g + 1) * HD]
                    s = lax.dot_general(q, keys, (((1,), (1,)), ((), ())), preferred_element_type=F32)
                    p = jnp.exp2(s * log_scale + shut)
                    p_s[g, :, ks] = p.astype(BF16)
                    pu = p * uc[g : g + 1, ks]
                    den_a[g] += p[:, :BLK] + p[:, BLK:]
                    rho_a[g] += pu[:, :BLK] + pu[:, BLK:]
                return 0

            lax.fori_loop(0, chunks, weigh, 0)
            total = jnp.zeros((BLK, 1), F32)
            for g in range(GROUP):
                den = jnp.sum(den_a[g], axis=-1, keepdims=True)
                rho = jnp.sum(rho_a[g], axis=-1, keepdims=True) / den
                total += rho
                rho_b[g] = jnp.broadcast_to(rho, (BLK, HD)).astype(BF16)
                den_a[g] = jnp.broadcast_to(scale / den, (BLK, HD))
            sc_ref[pl.ds(inner, 1), :] += jnp.broadcast_to(total, (BLK, HD)).T[0:1, :]

            def spread(c, _):
                ks = pl.ds(pl.multiple_of(c * 2 * BLK, 2 * BLK), 2 * BLK)
                keys = kc[ks, :]
                for g in range(GROUP):
                    r = rho_b[g]
                    u = ub[g : g + 1, ks]
                    p = p_s[g, :, ks]
                    w = jnp.concatenate([p[:, :BLK] * (u[:, :BLK] - r), p[:, BLK:] * (u[:, BLK:] - r)], axis=1)
                    acc[g] += jnp.dot(w, keys, preferred_element_type=F32)
                return 0

            lax.fori_loop(0, chunks, spread, 0)
            for g in range(GROUP):
                outs[side][rows, g * HD : (g + 1) * HD] = (acc[g] * den_a[g]).astype(BF16)


def attention(half, docs, mask, mask_in, place, queries, queries_in, keys, gains, before):
    rows = queries.shape[0]

    def whole(shape):
        return pl.BlockSpec(shape, lambda i, *_, n=len(shape): (0,) * n)

    head_block = pl.BlockSpec((rows, HEADS), lambda i, seg, mask, mask_in, place: (0, 2 * place[2] + half))
    extra = [before] if half else []
    return pl.pallas_call(
        functools.partial(attention_kernel, half),
        out_shape=(
            jax.ShapeDtypeStruct((rows, HEADS), BF16),
            jax.ShapeDtypeStruct((rows, HEADS), BF16),
            jax.ShapeDtypeStruct((8, BLK), F32),
        ),
        grid_spec=pltpu.PrefetchScalarGridSpec(
            num_scalar_prefetch=4,
            grid=(1,),
            in_specs=[whole((16, BLK)), head_block, head_block]
            + [whole(v.shape) for v in (*keys, *gains)]
            + [whole((8, BLK))] * half,
            out_specs=[whole((rows, HEADS)), whole((rows, HEADS)), whole((8, BLK))],
            scratch_shapes=[
                pltpu.VMEM((WINDOW, HD), BF16),
                pltpu.VMEM((GROUP, WINDOW), F32),
                pltpu.VMEM((BLK, WINDOW), F32),
                pltpu.VMEM((GROUP, BLK, WINDOW), BF16),
                pltpu.VMEM((GROUP, BLK, BLK), F32),
                pltpu.VMEM((GROUP, BLK, BLK), F32),
                pltpu.VMEM((GROUP, BLK, BLK), BF16),
                pltpu.VMEM((GROUP, BLK, HD), F32),
                pltpu.VMEM((GROUP, WINDOW), BF16),
                pltpu.SMEM((16,), jnp.int32),
            ],
        ),
        compiler_params=limit(24),
        cost_estimate=pl.CostEstimate(flops=5 * 10**9, bytes_accessed=3 << 20, transcendentals=5 * 10**6),
        name="attention",
    )(docs, mask, mask_in, place, docs.reshape(16, BLK), queries, queries_in, *keys, *gains, *extra)


def scale_kernel(place_s, near_ref, reward_ref, critic_ref, own_ref, live_ref, *refs):
    parts, o_ref = refs[:4], refs[4]
    section, core = place_s[3], place_s[2]
    b = pl.program_id(0)
    row = pl.ds(2 * core + b, 1)
    own, near = own_ref[row, :], near_ref[row, :]
    actor_term = penalty_weight * (own - near) - (reward_ref[row, :] - critic_ref[row, :])
    critic_term = own - near
    loss = jnp.where(section == 0, actor_term, jnp.where(section == 3, critic_term, 0.0))
    loss = live_ref[pl.ds(b, 1), :].astype(F32) * loss
    factor = jnp.broadcast_to(loss, (BLK, BLK)).T
    for number, ref in enumerate(parts):
        kv = 2 * core + number if number < 2 else 2 * (1 - core) + number - 2
        for g in range(GROUP):
            lanes = pl.ds(pl.multiple_of((kv * GROUP + g) * HD, HD), HD)
            o_ref[:, lanes] = (ref[:, g * HD : (g + 1) * HD].astype(F32) * factor).astype(BF16)


def scaled(place, near, reward, critic, own, live, parts):
    rows = parts[0].shape[0]

    def whole(shape):
        return pl.BlockSpec(shape, lambda i, place, n=len(shape): (0,) * n)

    return pl.pallas_call(
        scale_kernel,
        out_shape=jax.ShapeDtypeStruct((rows, QH * HD), BF16),
        grid_spec=pltpu.PrefetchScalarGridSpec(
            num_scalar_prefetch=1,
            grid=(2,),
            in_specs=[whole((8, BLK))] * 4
            + [whole((2, BLK))]
            + [pl.BlockSpec((BLK, HEADS), lambda i, place: (i, 0))] * 4,
            out_specs=pl.BlockSpec((BLK, QH * HD), lambda i, place: (i, 0)),
        ),
        compiler_params=limit(12),
        name="scaled",
    )(place, near, reward, critic, own, live, *parts)


def gathered_weights(part_a, part_b):
    a_own = stack([part_a, x_shift(part_a, 1), x_shift(part_a, -1), x_shift(part_a, 2)])
    b_back, b_ahead = [part_b], [part_b]
    for _ in range(3):
        b_back.append(z_shift(b_back[-1], 1))
        b_ahead.append(z_shift(b_ahead[-1], -1))
    b_back.append(z_shift(b_back[-1], 1))
    turns = [v for pair in zip(b_back[1:4], b_ahead[1:]) for v in pair]
    b_own = stack([part_b] + turns + b_back[4:])
    all_a = [a_own]
    a_back, a_ahead = a_own, a_own
    for _ in range(3):
        a_back, a_ahead = z_shift(a_back, 1), z_shift(a_ahead, -1)
        all_a += [a_back, a_ahead]
    all_a += [z_shift(a_back[:2], 1), z_shift(a_ahead[2:], -1)]
    b_one, b_three = x_shift(b_own, 1), x_shift(b_own, -1)
    all_b = [b_own, b_one, b_three, x_shift(b_one[:4], 1), x_shift(b_three[4:], -1)]
    return all_a + all_b


def after(value, *others):
    return lax.optimization_barrier((value, *others))[0]


def chip_shift(value, step):
    return plane_permute(value, lambda x, z, core: (x, z + step, core) if z % Z_LOW + step < Z_LOW else None)


def key_window(packed):
    return [packed, chip_shift(packed, 1), chip_shift(packed, 2)]


def on_device(hidden, queries, kv_weight, readout, segments, block_mask, response):
    fsdp = lax.axis_index("fsdp")
    seq = lax.axis_index("seq")
    section = lax.axis_index("section")
    chip, core = seq // 2, seq % 2
    place = jnp.stack([fsdp // 2, (fsdp % 2) * Z_LOW + chip, core, section])
    mask = block_mask[0].reshape(-1)
    parts_of_weight = pack_weights(place, pltpu.with_memory_space_constraint(kv_weight[0], pltpu.HBM), readout[0].reshape(QH, HD))
    own_hidden = pltpu.with_memory_space_constraint(hidden[0], pltpu.HBM)
    own_queries = pltpu.with_memory_space_constraint(queries[0], pltpu.HBM)
    hidden_in = pltpu.with_memory_space_constraint(core_swap(hidden[0]), pltpu.HBM)
    weights = gathered_weights(*parts_of_weight)
    queries_in, mask_in = (core_swap(after(v, *weights)) for v in (queries[0], mask))
    mine, theirs = project(place, own_hidden, hidden_in, weights)
    keys_a, keys_b = (key_window(v) for v in finish(mine, core_swap(theirs)))
    queries_in = pltpu.with_memory_space_constraint(queries_in, pltpu.HBM)
    same = (segments[0], mask, mask_in, place, own_queries, queries_in)
    own_a, lent_a, sums_a = attention(0, *same, keys_a, keys_a, None)
    got_a = core_swap(lent_a)
    own_b, lent_b, sums = attention(1, *same, keys_b, keys_a, sums_a)
    totals = sums + core_swap(sums)
    near = lax.ppermute(totals, "section", [(1, 0), (2, 3)])
    reward = lax.ppermute(totals, "section", [(2, 0)])
    critic = lax.ppermute(totals, "section", [(3, 0)])
    got_b = core_swap(lent_b)
    scores = lax.dynamic_slice_in_dim(totals, 2 * core, 2).reshape(1, -1)
    live = response.reshape(2, BLK)
    query_grad = scaled(place, near, reward, critic, totals, live, [own_a, own_b, got_a, got_b])
    return (scores, query_grad[None])


def solution(mesh):
    placed = (
        P("section", ("fsdp", "seq"), None),
        P("section", ("fsdp", "seq"), None),
        P("section", ("fsdp", "seq"), None),
        P("section", None),
        P("fsdp", None),
        P("fsdp", "seq", None),
        P(("fsdp", "seq")),
    )
    return jax.shard_map(
        on_device,
        mesh=mesh,
        in_specs=placed,
        out_specs=(P("section", ("fsdp", "seq")), P("section", ("fsdp", "seq"), None)),
        check_vma=False,
    )
```

```python
import functools
import math

import jax
import jax.numpy as jnp
import numpy as np
from jax import lax
from jax.experimental import pallas as pl
from jax.experimental.pallas import tpu as pltpu
from jax.sharding import PartitionSpec as P

QH = 32
KVH = 4
HD = 128
BLK = 128
GROUP = QH // KVH
KVW = KVH * HD
HALF = KVW // 2
WINDOW = 12 * BLK
HEADS = GROUP * HD
ZORDER = (0, 7, 1, 6, 2, 5, 3, 4)
NEG = -1e30
PLANE = ("fsdp", "seq")
X_SIZE, Z_SIZE, Z_LOW = 4, 8, 4
F32 = jnp.float32
BF16 = jnp.bfloat16

penalty_weight = 0.5


def flat(x, z, core):
    return (x * (Z_SIZE // Z_LOW) + z // Z_LOW) * (2 * Z_LOW) + (z % Z_LOW) * 2 + core


def plane_permute(value, target):
    pairs = []
    for x in range(X_SIZE):
        for z in range(Z_SIZE):
            for core in range(2):
                there = target(x, z, core)
                if there is not None:
                    pairs.append((flat(x, z, core), flat(*there)))
    return lax.ppermute(value, PLANE, pairs)


def x_shift(value, step):
    return plane_permute(value, lambda x, z, core: ((x + step) % X_SIZE, z, core))


def z_shift(value, step):
    return plane_permute(value, lambda x, z, core: (x, (z + step) % Z_SIZE, core))


def core_swap(value):
    return plane_permute(value, lambda x, z, core: (x, z, 1 - core))


def limit(mib):
    return pltpu.CompilerParams(vmem_limit_bytes=mib << 20)


def pack_kernel(place_s, w_ref, r_ref, a_ref, b_ref):
    core = place_s[2]
    order = [2 * core, 2 * core + 1, 2 - 2 * core, 3 - 2 * core]

    def lanes(kv):
        return pl.ds(pl.multiple_of(kv * HD, HD), HD)

    for n in range(2):
        a_ref[:, n * HD : (n + 1) * HD] = w_ref[:, lanes(order[2 * n])]
        b_ref[:BLK, n * HD : (n + 1) * HD] = w_ref[:, lanes(order[2 * n + 1])]
    gains = []
    for kv in order:
        gains.append(
            lax.dot_general(
                r_ref[pl.ds(pl.multiple_of(kv * GROUP, GROUP), GROUP), :],
                w_ref[:, pl.ds(pl.multiple_of(KVW + kv * HD, HD), HD)].astype(F32),
                (((1,), (1,)), ((), ())),
                precision=lax.Precision.HIGHEST,
                preferred_element_type=F32,
            )
        )
    b_ref[BLK:, :HD] = jnp.concatenate(gains[:2], axis=0).astype(BF16)
    b_ref[BLK:, HD:] = jnp.concatenate(gains[2:], axis=0).astype(BF16)


def pack_weights(place, weight, gains):
    def whole(shape):
        return pl.BlockSpec(shape, lambda i, place, n=len(shape): (0,) * n)

    shapes = [(BLK, HALF), (BLK + 16, HALF)]
    return pl.pallas_call(
        pack_kernel,
        out_shape=[jax.ShapeDtypeStruct(shape, BF16) for shape in shapes],
        grid_spec=pltpu.PrefetchScalarGridSpec(
            num_scalar_prefetch=1,
            grid=(1,),
            in_specs=[whole(weight.shape), whole(gains.shape)],
            out_specs=[whole(shape) for shape in shapes],
        ),
        compiler_params=limit(8),
        name="pack",
    )(place, weight, gains)


def stack_kernel(*refs):
    for i, ref in enumerate(refs[:-1]):
        refs[-1][i] = ref[...]


def stack(blocks):
    return pl.pallas_call(
        stack_kernel,
        out_shape=jax.ShapeDtypeStruct((len(blocks),) + blocks[0].shape, BF16),
        compiler_params=limit(8),
        name="stack",
    )(*blocks)


def project_kernel(place_s, own_ref, other_ref, *refs):
    all_a, all_b, refs = refs[:9], refs[9:14], refs[14:]
    mine_ref, theirs_ref, acc, gain_acc = refs
    now = pl.program_id(0)
    core = place_s[2]
    rows = own_ref.shape[0]
    tokens = 2 * rows
    for number in range(X_SIZE):

        @pl.when(now == number)
        def _():
            units = [(all_a[p], number) for p in range(7)] + [(all_a[7 + number // 2], number % 2)]
            w_a = jnp.concatenate([ref[i] for ref, i in units], axis=0)
            units = [(all_b[number + (i // 4 if number == 3 else 0)], i % (4 if number == 3 else 8)) for i in range(8)]
            w_b = jnp.concatenate([ref[i, :BLK, :] for ref, i in units], axis=0)
            wu = jnp.concatenate(
                [jnp.concatenate([ref[i, BLK:, :HD], ref[i, BLK:, HD:]], axis=0) for ref, i in units], axis=1
            )
            for side, ref in enumerate((own_ref, other_ref)):
                pieces = []
                for away in ZORDER:
                    z = (place_s[1] + away) % Z_SIZE
                    pieces.append(ref[:, pl.ds(pl.multiple_of((2 * z + core) * BLK, BLK), BLK)])
                h = jnp.concatenate(pieces, axis=1)
                for n, w in enumerate((w_a, w_b)):
                    part = jnp.dot(h, w, preferred_element_type=F32)
                    acc[side, n] = part if number == 0 else acc[side, n] + part
                part = lax.dot_general(wu, h, (((1,), (1,)), ((), ())), preferred_element_type=F32)
                gain_acc[side] = part if number == 0 else gain_acc[side] + part

    @pl.when(now == X_SIZE - 1)
    def _():
        for side in range(2):
            place_of = core if side == 0 else 1 - core
            for n, ref in enumerate((mine_ref, theirs_ref)):
                lanes = slice(n * HD, (n + 1) * HD)
                for half in range(2):
                    spot = pl.multiple_of(half * tokens + place_of * rows, rows)
                    ref[pl.ds(spot, rows), :] = acc[side, half, :, lanes]
                for i in range(rows // BLK):
                    spot = pl.multiple_of(2 * tokens + (2 * place_of + i) * 16, 16)
                    ref[pl.ds(spot, 16), :] = gain_acc[side, n * 16 : (n + 1) * 16, i * BLK : (i + 1) * BLK]


def project(place, own, other, weights):
    rows = own.shape[0]
    tokens = 2 * rows
    held = 2 * tokens + tokens // BLK * 16
    wide = 2 * Z_SIZE * BLK

    def whole(shape):
        return pl.BlockSpec(shape, lambda i, place, n=len(shape): (0,) * n)

    def column(i, place):
        return (0, (place[0] + jnp.where(i == 1, 3, jnp.where(i == 2, 1, jnp.where(i == 3, 2, 0)))) % X_SIZE)

    return pl.pallas_call(
        project_kernel,
        out_shape=[jax.ShapeDtypeStruct((held, HD), F32)] * 2,
        grid_spec=pltpu.PrefetchScalarGridSpec(
            num_scalar_prefetch=1,
            grid=(X_SIZE,),
            in_specs=[pl.BlockSpec((rows, wide), column)] * 2 + [whole(w.shape) for w in weights],
            out_specs=[whole((held, HD))] * 2,
            scratch_shapes=[pltpu.VMEM((2, 2, rows, HALF), F32), pltpu.VMEM((2, QH, rows), F32)],
        ),
        compiler_params=limit(28),
        cost_estimate=pl.CostEstimate(
            flops=2 * tokens * 32 * BLK * KVW, bytes_accessed=8 * tokens * 32 * BLK, transcendentals=0
        ),
        name="project",
    )(place, own, other, *weights)


def finish_kernel(mine_ref, in_ref, a_ref, b_ref):
    tokens = b_ref.shape[0]
    a_ref[:tokens, :] = (mine_ref[:tokens, :] + in_ref[:tokens, :]).astype(BF16)
    b_ref[...] = (mine_ref[tokens : 2 * tokens, :] + in_ref[tokens : 2 * tokens, :]).astype(BF16)
    u = mine_ref[2 * tokens :, :] + in_ref[2 * tokens :, :]
    a_ref[tokens:, :] = u.astype(BF16)


def finish(mine, received):
    tokens = 4 * BLK
    return pl.pallas_call(
        finish_kernel,
        out_shape=(
            jax.ShapeDtypeStruct((tokens + 64, HD), BF16),
            jax.ShapeDtypeStruct((tokens, HD), BF16),
        ),
        compiler_params=limit(8),
        name="finish",
    )(mine, received)


def attention_kernel(half, seg_s, mask_s, mask_in_s, place_s, docs_ref, *refs):
    queries, refs = refs[:2], refs[2:]
    key_refs, refs = refs[:3], refs[3:]
    gain_refs, refs = refs[:3], refs[3:]
    if half:
        before_ref, refs = refs[0], refs[1:]
    outs, sc_ref, refs = refs[:2], refs[2], refs[3:]
    kc, uc, bias, p_s, den_a, rho_a, rho_b, acc, ub, idx = refs
    log_scale = np.float32(math.log2(math.e) / math.sqrt(HD))
    scale = np.float32(1.0 / math.sqrt(HD))
    chip = place_s[1] % Z_LOW
    core = place_s[2]
    tokens = 4 * BLK
    sc_ref[...] = before_ref[...] if half else jnp.zeros_like(sc_ref)
    ii = lax.broadcasted_iota(jnp.int32, (BLK, BLK), 0)
    jj = lax.broadcasted_iota(jnp.int32, (BLK, BLK), 1)

    for side in range(2):
        side_core = core if side == 0 else 1 - core
        mask = (mask_s, mask_in_s)[side]
        for b in range(2):
            inner = 2 * side_core + b
            block = 4 * chip + inner
            first = seg_s[block * BLK]
            row_docs = jnp.broadcast_to(docs_ref[pl.ds(block, 1), :], (BLK, BLK)).astype(F32).T.astype(jnp.int32)

            def fetch(n, ref, gain_ref, at):
                d = pl.multiple_of(n * BLK, BLK)
                kc[pl.ds(d, BLK), :] = ref[pl.ds(pl.multiple_of(at * BLK, BLK), BLK), :]
                spot = tokens + at * 16
                high = gain_ref[pl.ds(pl.multiple_of(spot, 16), 16), :].astype(F32)
                uc[:, pl.ds(d, BLK)] = high[half * GROUP : (half + 1) * GROUP]

            n = jnp.int32(0)
            for back in (2, 1, 0):

                def scan(at, n, back=back):
                    key_block = 4 * (chip - back) + at
                    held = jnp.maximum(key_block, 0)
                    on = (key_block == block) | (
                        (key_block >= 0)
                        & (key_block < block)
                        & (mask[b * 16 + held] == 1)
                        & (seg_s[held * BLK + BLK - 1] == first)
                    )

                    @pl.when(on)
                    def _():
                        idx[n] = held
                        fetch(n, key_refs[back], gain_refs[back], at)

                    return n + on.astype(jnp.int32)

                n = lax.fori_loop(0, 4, scan, n)

            def fill(t, _):
                key_docs = docs_ref[pl.ds(idx[t], 1), :]
                bias[:, pl.ds(pl.multiple_of(t * BLK, BLK), BLK)] = jnp.where(row_docs == key_docs, 0.0, NEG)
                return 0

            lax.fori_loop(0, n - 1, fill, 0)
            last = pl.ds(pl.multiple_of((n - 1) * BLK, BLK), BLK)
            key_docs = docs_ref[pl.ds(block, 1), :]
            bias[:, last] = jnp.where((row_docs == key_docs) & (jj <= ii), 0.0, NEG)

            @pl.when(n % 2 == 1)
            def _():
                d = pl.ds(pl.multiple_of(n * BLK, BLK), BLK)
                bias[:, d] = jnp.full((BLK, BLK), NEG, F32)
                kc[d, :] = jnp.zeros((BLK, HD), BF16)
                uc[:, d] = jnp.zeros((GROUP, BLK), F32)

            chunks = (n + 1) // 2
            ub[...] = uc[...].astype(BF16)
            den_a[...] = jnp.zeros_like(den_a)
            rho_a[...] = jnp.zeros_like(rho_a)
            acc[...] = jnp.zeros_like(acc)
            rows = slice(b * BLK, (b + 1) * BLK)

            def weigh(c, _):
                ks = pl.ds(pl.multiple_of(c * 2 * BLK, 2 * BLK), 2 * BLK)
                keys = kc[ks, :]
                shut = bias[:, ks]
                for g in range(GROUP):
                    q = queries[side][rows, g * HD : (g + 1) * HD]
                    s = lax.dot_general(q, keys, (((1,), (1,)), ((), ())), preferred_element_type=F32)
                    p = jnp.exp2(s * log_scale + shut)
                    p_s[g, :, ks] = p.astype(BF16)
                    pu = p * uc[g : g + 1, ks]
                    den_a[g] += p[:, :BLK] + p[:, BLK:]
                    rho_a[g] += pu[:, :BLK] + pu[:, BLK:]
                return 0

            lax.fori_loop(0, chunks, weigh, 0)
            total = jnp.zeros((BLK, 1), F32)
            for g in range(GROUP):
                den = jnp.sum(den_a[g], axis=-1, keepdims=True)
                rho = jnp.sum(rho_a[g], axis=-1, keepdims=True) / den
                total += rho
                rho_b[g] = jnp.broadcast_to(rho, (BLK, HD)).astype(BF16)
                den_a[g] = jnp.broadcast_to(scale / den, (BLK, HD))
            sc_ref[pl.ds(inner, 1), :] += jnp.broadcast_to(total, (BLK, HD)).T[0:1, :]

            def spread(c, _):
                ks = pl.ds(pl.multiple_of(c * 2 * BLK, 2 * BLK), 2 * BLK)
                keys = kc[ks, :]
                for g in range(GROUP):
                    r = rho_b[g]
                    u = ub[g : g + 1, ks]
                    p = p_s[g, :, ks]
                    w = jnp.concatenate([p[:, :BLK] * (u[:, :BLK] - r), p[:, BLK:] * (u[:, BLK:] - r)], axis=1)
                    acc[g] += jnp.dot(w, keys, preferred_element_type=F32)
                return 0

            lax.fori_loop(0, chunks, spread, 0)
            for g in range(GROUP):
                outs[side][rows, g * HD : (g + 1) * HD] = (acc[g] * den_a[g]).astype(BF16)


def attention(half, docs, mask, mask_in, place, queries, queries_in, keys, gains, before):
    rows = queries.shape[0]

    def whole(shape):
        return pl.BlockSpec(shape, lambda i, *_, n=len(shape): (0,) * n)

    head_block = pl.BlockSpec((rows, HEADS), lambda i, seg, mask, mask_in, place: (0, 2 * place[2] + half))
    extra = [before] if half else []
    return pl.pallas_call(
        functools.partial(attention_kernel, half),
        out_shape=(
            jax.ShapeDtypeStruct((rows, HEADS), BF16),
            jax.ShapeDtypeStruct((rows, HEADS), BF16),
            jax.ShapeDtypeStruct((8, BLK), F32),
        ),
        grid_spec=pltpu.PrefetchScalarGridSpec(
            num_scalar_prefetch=4,
            grid=(1,),
            in_specs=[whole((16, BLK)), head_block, head_block]
            + [whole(v.shape) for v in (*keys, *gains)]
            + [whole((8, BLK))] * half,
            out_specs=[whole((rows, HEADS)), whole((rows, HEADS)), whole((8, BLK))],
            scratch_shapes=[
                pltpu.VMEM((WINDOW, HD), BF16),
                pltpu.VMEM((GROUP, WINDOW), F32),
                pltpu.VMEM((BLK, WINDOW), F32),
                pltpu.VMEM((GROUP, BLK, WINDOW), BF16),
                pltpu.VMEM((GROUP, BLK, BLK), F32),
                pltpu.VMEM((GROUP, BLK, BLK), F32),
                pltpu.VMEM((GROUP, BLK, BLK), BF16),
                pltpu.VMEM((GROUP, BLK, HD), F32),
                pltpu.VMEM((GROUP, WINDOW), BF16),
                pltpu.SMEM((16,), jnp.int32),
            ],
        ),
        compiler_params=limit(24),
        cost_estimate=pl.CostEstimate(flops=5 * 10**9, bytes_accessed=3 << 20, transcendentals=5 * 10**6),
        name="attention",
    )(docs, mask, mask_in, place, docs.reshape(16, BLK), queries, queries_in, *keys, *gains, *extra)


def scale_kernel(place_s, near_ref, reward_ref, critic_ref, own_ref, live_ref, *refs):
    parts, o_ref = refs[:4], refs[4]
    section, core = place_s[3], place_s[2]
    b = pl.program_id(0)
    row = pl.ds(2 * core + b, 1)
    own, near = own_ref[row, :], near_ref[row, :]
    actor_term = penalty_weight * (own - near) - (reward_ref[row, :] - critic_ref[row, :])
    critic_term = own - near
    loss = jnp.where(section == 0, actor_term, jnp.where(section == 3, critic_term, 0.0))
    loss = live_ref[pl.ds(b, 1), :].astype(F32) * loss
    factor = jnp.broadcast_to(loss, (BLK, BLK)).T
    for number, ref in enumerate(parts):
        kv = 2 * core + number if number < 2 else 2 * (1 - core) + number - 2
        for g in range(GROUP):
            lanes = pl.ds(pl.multiple_of((kv * GROUP + g) * HD, HD), HD)
            o_ref[:, lanes] = (ref[:, g * HD : (g + 1) * HD].astype(F32) * factor).astype(BF16)


def scaled(place, near, reward, critic, own, live, parts):
    rows = parts[0].shape[0]

    def whole(shape):
        return pl.BlockSpec(shape, lambda i, place, n=len(shape): (0,) * n)

    return pl.pallas_call(
        scale_kernel,
        out_shape=jax.ShapeDtypeStruct((rows, QH * HD), BF16),
        grid_spec=pltpu.PrefetchScalarGridSpec(
            num_scalar_prefetch=1,
            grid=(2,),
            in_specs=[whole((8, BLK))] * 4
            + [whole((2, BLK))]
            + [pl.BlockSpec((BLK, HEADS), lambda i, place: (i, 0))] * 4,
            out_specs=pl.BlockSpec((BLK, QH * HD), lambda i, place: (i, 0)),
        ),
        compiler_params=limit(12),
        name="scaled",
    )(place, near, reward, critic, own, live, *parts)


def gathered_weights(part_a, part_b):
    a_own = stack([part_a, x_shift(part_a, 1), x_shift(part_a, -1), x_shift(part_a, 2)])
    b_back, b_ahead = [part_b], [part_b]
    for _ in range(3):
        b_back.append(z_shift(b_back[-1], 1))
        b_ahead.append(z_shift(b_ahead[-1], -1))
    b_back.append(z_shift(b_back[-1], 1))
    turns = [v for pair in zip(b_back[1:4], b_ahead[1:]) for v in pair]
    b_own = stack([part_b] + turns + b_back[4:])
    all_a = [a_own]
    a_back, a_ahead = a_own, a_own
    for _ in range(3):
        a_back, a_ahead = z_shift(a_back, 1), z_shift(a_ahead, -1)
        all_a += [a_back, a_ahead]
    all_a += [z_shift(a_back[:2], 1), z_shift(a_ahead[2:], -1)]
    b_one, b_three = x_shift(b_own, 1), x_shift(b_own, -1)
    all_b = [b_own, b_one, b_three, x_shift(b_one[:4], 1), x_shift(b_three[4:], -1)]
    return all_a + all_b


def after(value, *others):
    return lax.optimization_barrier((value, *others))[0]


def chip_shift(value, step):
    return plane_permute(value, lambda x, z, core: (x, z + step, core) if z % Z_LOW + step < Z_LOW else None)


def key_window(packed):
    return [packed, chip_shift(packed, 1), chip_shift(packed, 2)]


def on_device(hidden, queries, kv_weight, readout, segments, block_mask, response):
    fsdp = lax.axis_index("fsdp")
    seq = lax.axis_index("seq")
    section = lax.axis_index("section")
    chip, core = seq // 2, seq % 2
    place = jnp.stack([fsdp // 2, (fsdp % 2) * Z_LOW + chip, core, section])
    mask = block_mask[0].reshape(-1)
    parts_of_weight = pack_weights(place, pltpu.with_memory_space_constraint(kv_weight[0], pltpu.HBM), readout[0].reshape(QH, HD))
    own_hidden = pltpu.with_memory_space_constraint(hidden[0], pltpu.HBM)
    own_queries = pltpu.with_memory_space_constraint(queries[0], pltpu.HBM)
    hidden_in = pltpu.with_memory_space_constraint(core_swap(hidden[0]), pltpu.HBM)
    weights = gathered_weights(*parts_of_weight)
    queries_in, mask_in = (core_swap(after(v, *weights)) for v in (queries[0], mask))
    mine, theirs = project(place, own_hidden, hidden_in, weights)
    keys_a, keys_b = (key_window(v) for v in finish(mine, core_swap(theirs)))
    queries_in = pltpu.with_memory_space_constraint(queries_in, pltpu.HBM)
    same = (segments[0], mask, mask_in, place, own_queries, queries_in)
    own_a, lent_a, sums_a = attention(0, *same, keys_a, keys_a, None)
    got_a = core_swap(lent_a)
    own_b, lent_b, sums = attention(1, *same, keys_b, keys_a, sums_a)
    totals = sums + core_swap(sums)
    near = lax.ppermute(totals, "section", [(1, 0), (2, 3)])
    reward = lax.ppermute(totals, "section", [(2, 0)])
    critic = lax.ppermute(totals, "section", [(3, 0)])
    got_b = core_swap(lent_b)
    scores = lax.dynamic_slice_in_dim(totals, 2 * core, 2).reshape(1, -1)
    live = response.reshape(2, BLK)
    query_grad = scaled(place, near, reward, critic, totals, live, [own_a, own_b, got_a, got_b])
    return (scores, query_grad[None])


def solution(mesh):
    placed = (
        P("section", ("fsdp", "seq"), None),
        P("section", ("fsdp", "seq"), None),
        P("section", ("fsdp", "seq"), None),
        P("section", None),
        P("fsdp", None),
        P("fsdp", "seq", None),
        P(("fsdp", "seq")),
    )
    return jax.shard_map(
        on_device,
        mesh=mesh,
        in_specs=placed,
        out_specs=(P("section", ("fsdp", "seq")), P("section", ("fsdp", "seq"), None)),
        check_vma=False,
    )
```
